32 devices in a mesh: groups: 2 (over y), epoch: 4 (over z), space: 2 (over x), sub: 2 (over core).
Axes of the slice: x: 2, y: 2, z: 4, core: 2. Of those that a mesh axis runs over, the one named last changes fastest.
Arguments:
- slc: bfloat16 [2, 64, 128, 1024], P(None, ('groups', 'epoch'), 'space', 'sub'), parts along dimension 1, may hold values from -8 to 8
- offsets: int32 [64, 4], P(('groups', 'epoch')), parts along dimension 0, may hold values from 1 to 8, as said below
- weights: float32 [64, 4], P(('groups', 'epoch')), parts along dimension 0, may hold values from 0.3 to 3
- estimate: float32 [64, 32, 1024], P(('groups', 'epoch'), 'space', 'sub'), parts along dimension 0, may hold values from -2 to 2
- direction: float32 [64, 32, 1024], P(('groups', 'epoch'), 'space', 'sub'), parts along dimension 0, may hold values from -2 to 2
- prev_mean: float32 [1], replicated, may hold values from 0.05 to 0.5
Outputs:
- new_estimate: float32 [64, 32, 1024], P(('groups', 'epoch'), 'space', 'sub'), parts along dimension 0
- new_direction: float32 [64, 32, 1024], P(('groups', 'epoch'), 'space', 'sub'), parts along dimension 0
The draws below stay inside these ranges and needn't reach their ends.
There are 2 independent parts, one for each index of `groups`. The reference program is written for one: setup_inputs(seed, part) draws one part's arguments, and reference() takes and returns one part's arrays. A program takes and returns all parts, laid end to end along the dimension named above; an argument that names none is the same for every part. Nothing has to cross between parts.
Inputs may be any that keep to these rules, and one draw needn't show every extreme that they name: `offsets`: each row holds 4 different distances; partners wrap past the last epoch to the first.
All inputs are finite; a program needn't handle non-finite values.
Results may differ from the reference program's by a relative error of at most 0.0003.
Values may be sent and summed in bfloat16 or wider, within the bound.
A program may use at most 64 MiB of HBM per device.

```python
import math
import jax
import jax.numpy as jnp
from jax import lax

SLOTS = 4
OFFS = 8
LOOK = 4
RADIUS = 3
EPOCHS = 32
ROWS = 128
COLS = 1024


def draw_slc(key, part):
    keys = jax.random.split(jax.random.fold_in(key, 7), 6)
    scene_real = jax.random.normal(keys[0], (ROWS, COLS), jnp.float32) * math.sqrt(0.5)
    scene_imag = jax.random.normal(keys[1], (ROWS, COLS), jnp.float32) * math.sqrt(0.5)
    offset_phase = jax.random.uniform(keys[2], (EPOCHS, 1, 1), jnp.float32, -math.pi, math.pi)
    jitter = 0.4 * jax.random.normal(keys[3], (EPOCHS, ROWS, COLS), jnp.float32)
    noise_level = jnp.exp(jax.random.uniform(keys[4], (EPOCHS, 1, 1), jnp.float32, math.log(0.2), math.log(3.0)))
    noise = jax.random.normal(keys[5], (2, EPOCHS, ROWS, COLS), jnp.float32) * math.sqrt(0.5) * noise_level
    phase = offset_phase + jitter
    cosine = jnp.cos(phase)
    sine = jnp.sin(phase)
    real_part = scene_real * cosine - scene_imag * sine + noise[0]
    imag_part = scene_real * sine + scene_imag * cosine + noise[1]
    stacked = jnp.stack([real_part, imag_part])
    return jnp.clip(stacked, -8.0, 8.0).astype(jnp.bfloat16)


def leading(row_values, wanted):
    position = jnp.argmax(row_values == wanted)
    return jnp.roll(row_values, -position)


def draw_offsets(key, part):
    keys = jax.random.split(jax.random.fold_in(key, 11), EPOCHS)
    ordered = jax.vmap(lambda single: jax.random.permutation(single, OFFS))(keys) + 1
    ordered = ordered.astype(jnp.int32)
    ordered = ordered.at[0].set(leading(ordered[0], OFFS))
    ordered = ordered.at[1].set(leading(ordered[1], 1))
    return ordered[:, :SLOTS].astype(jnp.int32)


def shard_levels(own_key, dims, cuts, smallest, largest):
    def one(dim, shards_of):
        draws = jax.random.uniform(jax.random.fold_in(jax.random.fold_in(own_key, 6), dim), (shards_of,), jnp.float32, smallest / len(cuts), largest / len(cuts))
        return jnp.repeat(jnp.exp(draws), dims[dim] // shards_of).reshape((-1,) + (1,) * (len(dims) - dim - 1))

    loudness = one(*cuts[0])
    for cut in cuts[1:]:
        loudness = loudness * one(*cut)
    return loudness


def normal_values(own_key, shape, scale, most, shards=(), kind=jnp.bfloat16):
    drawn = jax.random.normal(own_key, shape, jnp.float32) * scale
    if len(shards) > 0:
        drawn = shard_levels(own_key, shape, shards, -0.22, 0.18) * drawn
    return jnp.clip(drawn, min=-most, max=most).astype(kind)


def setup_inputs(seed: int = 0, part: int = 0) -> dict:
    key_list = jax.random.split(jax.random.key(seed), 7)
    part_splits = jax.random.split(jax.random.fold_in(key_list[6], part), 7)
    slc = draw_slc(jax.random.fold_in(jax.random.fold_in(key_list[6], part), 71), part)
    offsets = draw_offsets(jax.random.fold_in(jax.random.fold_in(key_list[6], part), 71), part)
    weights = jnp.clip(jnp.exp(math.log(3.0) - 2.3025851 * jax.random.uniform(part_splits[2], (EPOCHS, SLOTS), jnp.float32) ** shard_levels(part_splits[2], (EPOCHS, SLOTS), ((0, 4),), -0.2, 0.2)), 0.3, 3.0)
    estimate = normal_values(part_splits[3], (EPOCHS, ROWS // LOOK, COLS), 0.3, 2.0, ((0, 4), (1, 2), (2, 2)), jnp.float32)
    direction = normal_values(part_splits[4], (EPOCHS, ROWS // LOOK, COLS), 0.3, 2.0, ((0, 4), (1, 2), (2, 2)), jnp.float32)
    prev_mean = jnp.clip(jnp.exp(jax.random.uniform(key_list[5], (1,), jnp.float32, math.log(0.05), math.log(0.5))), 0.05, 0.5)
    return dict(slc=slc, offsets=offsets, weights=weights, estimate=estimate, direction=direction, prev_mean=prev_mean)


EPSILON = 1e-06

def looked_sum(field):
    shape = field.shape
    return lax.optimization_barrier(jnp.sum(field.reshape(shape[:-2] + (shape[-2] // LOOK, LOOK, shape[-1])), axis=-2))

def window_sum(padded, axis):
    length = padded.shape[axis] - 2 * RADIUS
    total = lax.slice_in_dim(padded, 0, length, axis=axis)
    for shift_at in range(1, 2 * RADIUS + 1):
        total = total + lax.slice_in_dim(padded, shift_at, shift_at + length, axis=axis)
    return total

def box_sum(field):
    widths = [(0, 0)] * (field.ndim - 2) + [(RADIUS, RADIUS), (RADIUS, RADIUS)]
    padded = jnp.pad(field, widths)
    return window_sum(window_sum(padded, field.ndim - 2), field.ndim - 1)

def reference(slc, offsets, weights, estimate, direction, prev_mean):
    numbers = jnp.arange(EPOCHS, dtype=jnp.int32)
    partner = ((numbers[:, None] + offsets) % EPOCHS).astype(jnp.int32)

    def one_epoch(epoch_index):
        own_real = slc[0, epoch_index].astype(jnp.float32)
        own_imag = slc[1, epoch_index].astype(jnp.float32)
        powers = looked_sum(own_real * own_real + own_imag * own_imag)
        pieces = []
        for slot_index in range(SLOTS):
            mate_index = partner[epoch_index, slot_index]
            mate_real = slc[0, mate_index].astype(jnp.float32)
            mate_imag = slc[1, mate_index].astype(jnp.float32)
            pieces.append(looked_sum(own_real * mate_real + own_imag * mate_imag))
            pieces.append(looked_sum(own_imag * mate_real - own_real * mate_imag))
        return (jnp.stack(pieces), powers)
    looked, powers = lax.map(one_epoch, numbers)
    boxed = box_sum(looked)
    power_box = box_sum(powers)
    coh_real = boxed[:, 0::2]
    coh_imag = boxed[:, 1::2]
    denominator = power_box[:, None] * power_box[partner] + EPSILON
    coherence = (coh_real * coh_real + coh_imag * coh_imag) / denominator
    observed = coh_imag / jnp.sqrt(denominator)
    fitted = estimate[:, None] - estimate[partner]
    factor = weights[:, :, None, None] * coherence
    weighted = factor * (observed - fitted)
    gradient = lax.optimization_barrier(jnp.sum(weighted, axis=1)) - jax.ops.segment_sum(weighted.reshape((-1,) + weighted.shape[2:]), partner.reshape(-1), num_segments=EPOCHS)
    cell_count = float(EPOCHS * (ROWS // LOOK) * COLS)
    grad_norm = jnp.sum(gradient * gradient)
    crossed = jnp.sum(gradient * direction)
    momentum = grad_norm / cell_count / prev_mean[0]
    new_direction = gradient + momentum * direction
    along_sum = grad_norm + momentum * crossed
    spread = new_direction[:, None] - new_direction[partner]
    curvature = jnp.sum(factor * spread * spread)
    step_size = along_sum / curvature
    return (estimate + step_size * new_direction, new_direction)
```

```python
import functools

import jax
import jax.numpy as jnp
from jax import lax
from jax.experimental import pallas as pl
from jax.experimental.pallas import tpu as pltpu
from jax.sharding import PartitionSpec as P

SLOTS = 4
OFFS = 8
LOOK = 4
RADIUS = 3
EPSILON = 1e-06
LANES = 128
PACK = 16
MESH = pl.DeviceIdType.MESH
F32 = jnp.float32
BF16 = jnp.bfloat16


def windowed(x, axis):
    size = x.shape[axis]
    three = x + pltpu.roll(x, 1, axis) + pltpu.roll(x, size - 1, axis)
    return x + pltpu.roll(three, 2, axis) + pltpu.roll(three, size - 2, axis)


def folded(x):
    total = None
    for row in range(0, x.shape[0], 8):
        for col in range(0, x.shape[1], LANES):
            piece = x[row : row + 8, col : col + LANES]
            total = piece if total is None else total + piece
    return total


def step_kernel(
    sizes,
    slc,
    offsets,
    weights,
    estimate,
    direction,
    prev_mean,
    new_estimate,
    new_direction,
    raw,
    tmp,
    ext,
    pbox,
    est,
    dirs,
    dir_low,
    dir_in,
    acc,
    ret_in,
    own_low,
    own_in,
    grad,
    factors,
    red_c,
    red_x,
    red_z,
    loc_sem,
    misc_sem,
    z_send,
    z_recv,
    e_send,
    e_recv,
    d_sem,
    x_send,
    x_recv,
    c_send,
    c_recv,
    r_send,
    r_recv,
    o_send,
    o_recv,
    rc_send,
    rc_recv,
    rx_send,
    rx_recv,
    rz_send,
    rz_recv,
):
    nz, nx, nc = sizes
    here = slc.shape[1]
    rows = slc.shape[2]
    cols = slc.shape[3]
    total_rows = rows + 2 * PACK
    look_rows = rows // LOOK
    ext_rows = total_rows // LOOK
    rim_rows = PACK // LOOK
    blocks = cols // LANES + 1
    everything = here + OFFS
    z = lax.axis_index("epoch")
    x = lax.axis_index("space")
    c = lax.axis_index("sub")
    z_prev = {"epoch": lax.rem(z + nz - 1, nz)}
    z_next = {"epoch": lax.rem(z + 1, nz)}
    has_next = x < nx - 1
    has_prev = x > 0

    local = [
        pltpu.make_async_copy(estimate, est.at[pl.ds(0, here)], misc_sem.at[0]),
        pltpu.make_async_copy(direction, dirs.at[pl.ds(0, here)], misc_sem.at[1]),
    ]

    def tile_in(b):
        return pltpu.make_async_copy(
            slc.at[:, b], raw.at[b, :, pl.ds(0, rows), pl.ds(0, cols)], loc_sem.at[b]
        )

    local[1].start()
    local[0].start()
    for b in range(here):
        tile_in(b).start()

    barrier = pltpu.get_barrier_semaphore()
    for axis, size, me in (("epoch", nz, z), ("space", nx, x), ("sub", nc, c)):
        for by in range(1, size):
            pl.semaphore_signal(
                barrier, inc=1, device_id={axis: lax.rem(me + by, size)}, device_id_type=MESH
            )
    pl.semaphore_wait(barrier, nz + nx + nc - 3)

    def remote(src, dst, send, recv, device):
        return pltpu.make_async_remote_copy(
            src_ref=src,
            dst_ref=dst,
            send_sem=send,
            recv_sem=recv,
            device_id=device,
            device_id_type=MESH,
        )

    def z_tile(k):
        return remote(
            slc.at[:, k],
            raw.at[here + k, :, pl.ds(0, rows), pl.ds(0, cols)],
            z_send.at[k],
            z_recv.at[k],
            z_prev,
        )

    def z_est(k):
        return remote(estimate.at[k], est.at[here + k], e_send.at[k], e_recv.at[k], z_prev)

    def z_dir():
        return remote(dir_low, dir_in, d_sem.at[0], d_sem.at[1], z_prev)

    def x_down(b, own):
        at = pl.ds(rows - PACK, PACK)
        src = slc.at[:, b, at] if own else raw.at[b, :, at, pl.ds(0, cols)]
        return remote(
            src,
            raw.at[b, :, pl.ds(rows + PACK, PACK), pl.ds(0, cols)],
            x_send.at[0, b],
            x_recv.at[0, b],
            {"space": lax.rem(x + 1, nx)},
        )

    def x_up(b, own):
        at = pl.ds(0, PACK)
        src = slc.at[:, b, at] if own else raw.at[b, :, at, pl.ds(0, cols)]
        return remote(
            src,
            raw.at[b, :, pl.ds(rows, PACK), pl.ds(0, cols)],
            x_send.at[1, b],
            x_recv.at[1, b],
            {"space": lax.rem(x + nx - 1, nx)},
        )

    def c_rim(b):
        start = pl.multiple_of((nc - 1 - c) * (cols - LANES), LANES)
        return remote(
            raw.at[b, :, :, pl.ds(start, LANES)],
            raw.at[b, :, :, pl.ds(cols, LANES)],
            c_send.at[b],
            c_recv.at[b],
            {"sub": lax.rem(c + 1, nc)},
        )

    def x_start(b, own):
        if nx > 1:
            pl.when(has_next)(lambda: x_down(b, own).start())
            pl.when(has_prev)(lambda: x_up(b, own).start())

    def x_wait(b, own):
        if nx > 1:
            pl.when(has_prev)(lambda: x_down(b, own).wait_recv())
            pl.when(has_next)(lambda: x_up(b, own).wait_recv())

    def x_drain(b, own):
        if nx > 1:
            pl.when(has_next)(lambda: x_down(b, own).wait_send())
            pl.when(has_prev)(lambda: x_up(b, own).wait_send())

    def returned(k):
        return remote(acc.at[here + k], ret_in.at[k], r_send.at[k], r_recv.at[k], z_next)

    def owned(k):
        return remote(own_low.at[k], own_in.at[k], o_send.at[k], o_recv.at[k], z_prev)

    for k in range(OFFS):
        x_start(k, True)
    for k in range(OFFS):
        z_est(k).start()
        z_tile(k).start()
    local[1].wait()
    dir_low[...] = dirs[pl.ds(0, OFFS)].astype(BF16)
    acc[...] = jnp.zeros_like(acc)
    local[0].wait()

    row_at = lax.broadcasted_iota(jnp.int32, (ext_rows, LANES), 0)
    lane_at = lax.broadcasted_iota(jnp.int32, (ext_rows, LANES), 1)
    row_first = jnp.where(has_prev, look_rows + rim_rows, ext_rows)
    row_last = jnp.where(has_next, look_rows + rim_rows, look_rows)
    row_ok = (row_at < row_last) | (row_at >= row_first)
    if nc > 1:
        lane_first = jnp.where(c == 0, LANES, LANES - RADIUS)
        lane_last = jnp.where(c == 0, RADIUS, 0)
        rim_ok = row_ok & ((lane_at < lane_last) | (lane_at >= lane_first))
    else:
        rim_ok = row_at < 0

    def boxed(field):
        return windowed(windowed(field, 0)[:look_rows], 1)[:, :cols]

    def prepare(b):
        for part in range(2):
            for v in range(blocks):
                tmp[part, v] = raw[b, part, :, v * LANES : (v + 1) * LANES].astype(F32)
        powers = []
        for v in range(blocks):
            keep = rim_ok if v == blocks - 1 else row_ok
            power = jnp.zeros((ext_rows, LANES), F32)
            for part in range(2):
                for look in range(LOOK):
                    value = tmp[part, v, pl.ds(look, ext_rows, stride=LOOK), :]
                    value = jnp.where(keep, value, 0.0)
                    ext[b, part, look, :, v * LANES : (v + 1) * LANES] = value
                    power = power + value * value
            powers.append(power)
        pbox[b] = boxed(jnp.concatenate(powers, axis=1))

    def pair(e, b):
        real = jnp.zeros((ext_rows, blocks * LANES), F32)
        imag = jnp.zeros((ext_rows, blocks * LANES), F32)
        for look in range(LOOK):
            own_real = ext[e, 0, look]
            own_imag = ext[e, 1, look]
            mate_real = ext[b, 0, look]
            mate_imag = ext[b, 1, look]
            real = real + (own_real * mate_real + own_imag * mate_imag)
            imag = imag + (own_imag * mate_real - own_real * mate_imag)
        real = boxed(real)
        imag = boxed(imag)
        distance = b - e
        weight = jnp.float32(0.0)
        for slot in range(SLOTS):
            weight = weight + jnp.where(
                offsets[e, slot] == distance, weights[e, slot], jnp.float32(0.0)
            )
        root = 1.0 / jnp.sqrt(pbox[e] * pbox[b] + EPSILON)
        real = real * root
        imag = imag * root
        factor = weight * (real * real + imag * imag)
        factors[e * (OFFS + 1) + distance] = factor
        weighted = factor * (imag - (est[e] - est[b]))
        acc[e] = acc[e] + weighted
        acc[b] = acc[b] - weighted

    def pairs_of(b):
        @pl.loop(lax.max(b - OFFS, 0), lax.min(b, here))
        def _(e):
            pair(e, b)

    def settle(b):
        k = b - here
        c_rim(b).wait_recv()
        prepare(b)
        z_est(k).wait_recv()
        pairs_of(b)
        own_low[k] = acc[k].astype(BF16)
        returned(k).start()
        owned(k).start()

    @pl.loop(0, here)
    def _(b):
        tile_in(b).wait()
        x_wait(b, True)
        c_rim(b).start()

        @pl.when(b > 0)
        def _():
            c_rim(b - 1).wait_recv()
            prepare(b - 1)
            pairs_of(b - 1)

    z_dir().start()
    c_rim(here - 1).wait_recv()
    prepare(here - 1)
    pairs_of(here - 1)

    @pl.loop(0, OFFS)
    def _(k):
        b = k + here
        z_tile(k).wait_recv()
        x_start(b, False)

        @pl.when(k > 0)
        def _():
            settle(b - 1)

        x_wait(b, False)
        c_rim(b).start()

    settle(everything - 1)

    z_dir().wait_recv()
    dirs[pl.ds(here, OFFS)] = dir_in[...].astype(F32)
    zero = jnp.zeros((8, LANES), F32)

    @pl.loop(OFFS, here)
    def _(k):
        grad[k] = acc[k]

    @pl.loop(0, OFFS)
    def _(k):
        returned(k).wait_recv()
        owned(k).wait_recv()
        grad[k] = acc[k] + ret_in[k]
        grad[here + k] = own_in[k].astype(F32) + acc[here + k]

    def one_epoch(e, sums):
        norm, crossed, gg, gd, dd = sums
        g = grad[e]
        d = dirs[e]
        norm = norm + folded(g * g)
        crossed = crossed + folded(g * d)
        for slot in range(SLOTS):
            far = offsets[e, slot]
            f = factors[e * (OFFS + 1) + far]
            dg = g - grad[e + far]
            ds = d - dirs[e + far]
            fg = f * dg
            gg = gg + folded(fg * dg)
            gd = gd + folded(fg * ds)
            dd = dd + folded(f * ds * ds)
        return norm, crossed, gg, gd, dd

    sums = lax.fori_loop(0, here, one_epoch, (zero,) * 5)
    tile_row = lax.broadcasted_iota(jnp.int32, (8, LANES), 0)
    tile = zero
    for index, value in enumerate(sums):
        whole = jnp.sum(jnp.sum(value, axis=0, keepdims=True), axis=1, keepdims=True)
        tile = jnp.where(tile_row == index, whole, tile)

    for axis, size, me, red, send, recv in (
        ("sub", nc, c, red_c, rc_send, rc_recv),
        ("space", nx, x, red_x, rx_send, rx_recv),
        ("epoch", nz, z, red_z, rz_send, rz_recv),
    ):
        if size == 1:
            continue
        red[me] = tile

        def share(by, source):
            return remote(
                red.at[source],
                red.at[source],
                send.at[by],
                recv.at[source],
                {axis: lax.rem(me + by, size)},
            )

        for by in range(1, size):
            share(by, me).start()
        for by in range(1, size):
            share(by, lax.rem(me + size - by, size)).wait_recv()
        for by in range(1, size):
            share(by, me).wait_send()
        tile = red[0]
        for source in range(1, size):
            tile = tile + red[source]

    grad_norm, crossed, grad_term, mixed_term, old_term = (tile[i : i + 1, 0:1] for i in range(5))
    cell_count = float(here * nz * look_rows * nx * cols * nc)
    momentum = grad_norm / cell_count / prev_mean[0]
    curvature = grad_term + 2.0 * momentum * mixed_term + momentum * momentum * old_term
    step = (grad_norm + momentum * crossed) / curvature

    @pl.loop(0, here)
    def _(e):
        moved = grad[e] + momentum * dirs[e]
        new_direction[e] = moved
        new_estimate[e] = est[e] + step * moved

    @pl.loop(0, OFFS)
    def _(k):
        z_tile(k).wait_send()
        z_est(k).wait_send()
        returned(k).wait_send()
        owned(k).wait_send()

    @pl.loop(0, here)
    def _(b):
        x_drain(b, True)

    @pl.loop(here, everything)
    def _(b):
        x_drain(b, False)

    @pl.loop(0, everything)
    def _(b):
        c_rim(b).wait_send()

    z_dir().wait_send()


def on_device(sizes, slc, offsets, weights, estimate, direction, prev_mean):
    nz, nx, nc = sizes
    here, rows, cols = slc.shape[1:]
    look_rows = rows // LOOK
    every = here + OFFS
    total_rows = rows + 2 * PACK
    ext_rows = total_rows // LOOK
    wide = cols + LANES
    grid_cell = (look_rows, cols)
    dma = pltpu.SemaphoreType.DMA
    scratch = [
        pltpu.VMEM((every, 2, total_rows, wide), BF16),
        pltpu.VMEM((2, wide // LANES, total_rows, LANES), F32),
        pltpu.VMEM((every, 2, LOOK, ext_rows, wide), F32),
        pltpu.VMEM((every,) + grid_cell, F32),
        pltpu.VMEM((every,) + grid_cell, F32),
        pltpu.VMEM((every,) + grid_cell, F32),
        pltpu.VMEM((OFFS,) + grid_cell, BF16),
        pltpu.VMEM((OFFS,) + grid_cell, BF16),
        pltpu.VMEM((every,) + grid_cell, F32),
        pltpu.VMEM((OFFS,) + grid_cell, F32),
        pltpu.VMEM((OFFS,) + grid_cell, BF16),
        pltpu.VMEM((OFFS,) + grid_cell, BF16),
        pltpu.VMEM((every,) + grid_cell, F32),
        pltpu.VMEM((here * (OFFS + 1),) + grid_cell, F32),
        pltpu.VMEM((nc, 8, LANES), F32),
        pltpu.VMEM((nx, 8, LANES), F32),
        pltpu.VMEM((nz, 8, LANES), F32),
        dma((here,)),
        dma((2,)),
        dma((OFFS,)),
        dma((OFFS,)),
        dma((OFFS,)),
        dma((OFFS,)),
        dma((2,)),
        dma((2, every)),
        dma((2, every)),
        dma((every,)),
        dma((every,)),
        dma((OFFS,)),
        dma((OFFS,)),
        dma((OFFS,)),
        dma((OFFS,)),
        dma((nc,)),
        dma((nc,)),
        dma((nx,)),
        dma((nx,)),
        dma((nz,)),
        dma((nz,)),
    ]
    anywhere = pl.BlockSpec(memory_space=pl.ANY)
    scalars = pl.BlockSpec(memory_space=pltpu.SMEM)
    vectors = pl.BlockSpec(memory_space=pltpu.VMEM)
    out = jax.ShapeDtypeStruct(estimate.shape, F32)
    return tuple(
        pl.pallas_call(
            functools.partial(step_kernel, sizes),
            name="cg_step",
            out_shape=(out, out),
            in_specs=[anywhere, scalars, scalars, anywhere, anywhere, scalars],
            out_specs=(vectors, vectors),
            scratch_shapes=scratch,
            compiler_params=pltpu.CompilerParams(
                collective_id=0, has_side_effects=True, vmem_limit_bytes=60 * 1024 * 1024
            ),
        )(slc, offsets, weights, estimate, direction, prev_mean)
    )


def solution(mesh):
    sizes = (mesh.shape["epoch"], mesh.shape["space"], mesh.shape["sub"])
    tile = P(("groups", "epoch"), "space", "sub")
    rows = P(("groups", "epoch"), None)
    return jax.shard_map(
        functools.partial(on_device, sizes),
        mesh=mesh,
        in_specs=(P(None, ("groups", "epoch"), "space", "sub"), rows, rows, tile, tile, P()),
        out_specs=(tile, tile),
        check_vma=False,
    )
```

```python
import functools

import jax
import jax.numpy as jnp
from jax import lax
from jax.experimental import pallas as pl
from jax.experimental.pallas import tpu as pltpu
from jax.sharding import PartitionSpec as P

SLOTS = 4
OFFS = 8
LOOK = 4
RADIUS = 3
EPSILON = 1e-06
LANES = 128
LAG = 3
PACK = 16
MESH = pl.DeviceIdType.MESH
F32 = jnp.float32
BF16 = jnp.bfloat16


def windowed(x, axis):
    size = x.shape[axis]
    three = x + pltpu.roll(x, 1, axis) + pltpu.roll(x, size - 1, axis)
    return x + pltpu.roll(three, 2, axis) + pltpu.roll(three, size - 2, axis)


def folded(x):
    total = None
    for row in range(0, x.shape[0], 8):
        for col in range(0, x.shape[1], LANES):
            piece = x[row : row + 8, col : col + LANES]
            total = piece if total is None else total + piece
    return total


def step_kernel(
    sizes,
    slc,
    offsets_in,
    weights_in,
    estimate,
    direction,
    gradient,
    totals,
    offsets,
    weights,
    raw,
    tmp,
    ext,
    pbox,
    est,
    dirs,
    dir_low,
    dir_in,
    acc,
    ret_in,
    own_low,
    own_in,
    grad,
    factors,
    red_s,
    red_z,
    loc_sem,
    misc_sem,
    z_send,
    z_recv,
    e_send,
    e_recv,
    d_sem,
    x_send,
    x_recv,
    c_send,
    c_recv,
    r_send,
    r_recv,
    o_send,
    o_recv,
    rs_send,
    rs_recv,
    rz_send,
    rz_recv,
):
    nz, nx, nc = sizes
    here = slc.shape[1]
    rows = slc.shape[2]
    cols = slc.shape[3]
    total_rows = rows + 2 * PACK
    look_rows = rows // LOOK
    ext_rows = total_rows // LOOK
    rim_rows = PACK // LOOK
    blocks = cols // LANES + 1
    everything = here + OFFS
    z = lax.axis_index("epoch")
    x = lax.axis_index("space")
    c = lax.axis_index("sub")
    z_prev = {"epoch": lax.rem(z + nz - 1, nz)}
    z_next = {"epoch": lax.rem(z + 1, nz)}
    has_next = x < nx - 1
    has_prev = x > 0

    local = [
        pltpu.make_async_copy(estimate, est.at[pl.ds(0, here)], misc_sem.at[0]),
        pltpu.make_async_copy(direction, dirs.at[pl.ds(0, here)], misc_sem.at[1]),
        pltpu.make_async_copy(offsets_in, offsets, misc_sem.at[2]),
        pltpu.make_async_copy(weights_in, weights, misc_sem.at[3]),
    ]

    def tile_in(b):
        return pltpu.make_async_copy(
            slc.at[:, b], raw.at[b, :, pl.ds(0, rows), pl.ds(0, cols)], loc_sem.at[b]
        )

    local[1].start()
    local[0].start()
    local[2].start()
    local[3].start()
    for b in range(here):
        tile_in(b).start()

    barrier = pltpu.get_barrier_semaphore()
    spread = nx * nc
    place = x * nc + c

    def along_z(by):
        return {"epoch": lax.rem(z + by, nz)}

    def in_plane(by):
        other = lax.rem(place + by, spread)
        return {"space": other // nc, "sub": lax.rem(other, nc)}

    for by in range(1, nz):
        pl.semaphore_signal(barrier, inc=1, device_id=along_z(by), device_id_type=MESH)
    for by in range(1, spread):
        pl.semaphore_signal(barrier, inc=1, device_id=in_plane(by), device_id_type=MESH)
    pl.semaphore_wait(barrier, nz + spread - 2)

    def remote(src, dst, send, recv, device):
        return pltpu.make_async_remote_copy(
            src_ref=src,
            dst_ref=dst,
            send_sem=send,
            recv_sem=recv,
            device_id=device,
            device_id_type=MESH,
        )

    def z_tile(k):
        return remote(
            slc.at[:, k],
            raw.at[here + k, :, pl.ds(0, rows), pl.ds(0, cols)],
            z_send.at[k],
            z_recv.at[k],
            z_prev,
        )

    def z_est(k):
        return remote(estimate.at[k], est.at[here + k], e_send.at[k], e_recv.at[k], z_prev)

    def z_dir():
        return remote(dir_low, dir_in, d_sem.at[0], d_sem.at[1], z_prev)

    def x_down(b, own):
        at = pl.ds(rows - PACK, PACK)
        src = slc.at[:, b, at] if own else raw.at[b, :, at, pl.ds(0, cols)]
        return remote(
            src,
            raw.at[b, :, pl.ds(rows + PACK, PACK), pl.ds(0, cols)],
            x_send.at[0, b],
            x_recv.at[0, b],
            {"space": lax.rem(x + 1, nx)},
        )

    def x_up(b, own):
        at = pl.ds(0, PACK)
        src = slc.at[:, b, at] if own else raw.at[b, :, at, pl.ds(0, cols)]
        return remote(
            src,
            raw.at[b, :, pl.ds(rows, PACK), pl.ds(0, cols)],
            x_send.at[1, b],
            x_recv.at[1, b],
            {"space": lax.rem(x + nx - 1, nx)},
        )

    def c_rim(b):
        start = pl.multiple_of((nc - 1 - c) * (cols - LANES), LANES)
        return remote(
            raw.at[b, :, :, pl.ds(start, LANES)],
            raw.at[b, :, :, pl.ds(cols, LANES)],
            c_send.at[b],
            c_recv.at[b],
            {"sub": lax.rem(c + 1, nc)},
        )

    def x_start(b, own):
        if nx > 1:
            pl.when(has_next)(lambda: x_down(b, own).start())
            pl.when(has_prev)(lambda: x_up(b, own).start())

    def x_wait(b, own):
        if nx > 1:
            pl.when(has_prev)(lambda: x_down(b, own).wait_recv())
            pl.when(has_next)(lambda: x_up(b, own).wait_recv())

    def x_drain(b, own):
        if nx > 1:
            pl.when(has_next)(lambda: x_down(b, own).wait_send())
            pl.when(has_prev)(lambda: x_up(b, own).wait_send())

    def returned(k):
        return remote(acc.at[here + k], ret_in.at[k], r_send.at[k], r_recv.at[k], z_next)

    def owned(k):
        return remote(own_low.at[k], own_in.at[k], o_send.at[k], o_recv.at[k], z_prev)

    for k in range(OFFS):
        x_start(k, True)
    for k in range(OFFS + LAG):
        if k < OFFS:
            z_tile(k).start()
        if k >= LAG:
            z_est(k - LAG).start()
    local[1].wait()
    dir_low[...] = dirs[pl.ds(0, OFFS)].astype(BF16)
    acc[...] = jnp.zeros_like(acc)
    for copy in (local[0], local[2], local[3]):
        copy.wait()
    z_dir().start()

    row_at = lax.broadcasted_iota(jnp.int32, (ext_rows, LANES), 0)
    lane_at = lax.broadcasted_iota(jnp.int32, (ext_rows, LANES), 1)
    row_first = jnp.where(has_prev, look_rows + rim_rows, ext_rows)
    row_last = jnp.where(has_next, look_rows + rim_rows, look_rows)
    row_ok = (row_at < row_last) | (row_at >= row_first)
    if nc > 1:
        lane_first = jnp.where(c == 0, LANES, LANES - RADIUS)
        lane_last = jnp.where(c == 0, RADIUS, 0)
        rim_ok = row_ok & ((lane_at < lane_last) | (lane_at >= lane_first))
    else:
        rim_ok = row_at < 0

    def boxed(field):
        return windowed(windowed(field, 0)[:look_rows], 1)[:, :cols]

    def prepare(b):
        for part in range(2):
            for v in range(blocks):
                tmp[part, v] = raw[b, part, :, v * LANES : (v + 1) * LANES].astype(F32)
        powers = []
        for v in range(blocks):
            keep = rim_ok if v == blocks - 1 else row_ok
            power = jnp.zeros((ext_rows, LANES), F32)
            for part in range(2):
                for look in range(LOOK):
                    value = tmp[part, v, pl.ds(look, ext_rows, stride=LOOK), :]
                    value = jnp.where(keep, value, 0.0)
                    ext[b, part, look, :, v * LANES : (v + 1) * LANES] = value
                    power = power + value * value
            powers.append(power)
        pbox[b] = boxed(jnp.concatenate(powers, axis=1))

    def pair(e, b):
        real = jnp.zeros((ext_rows, blocks * LANES), F32)
        imag = jnp.zeros((ext_rows, blocks * LANES), F32)
        for look in range(LOOK):
            own_real = ext[e, 0, look]
            own_imag = ext[e, 1, look]
            mate_real = ext[b, 0, look]
            mate_imag = ext[b, 1, look]
            real = real + (own_real * mate_real + own_imag * mate_imag)
            imag = imag + (own_imag * mate_real - own_real * mate_imag)
        real = boxed(real)
        imag = boxed(imag)
        distance = b - e
        weight = jnp.float32(0.0)
        for slot in range(SLOTS):
            weight = weight + jnp.where(
                offsets[e, slot] == distance, weights[e, slot], jnp.float32(0.0)
            )
        root = 1.0 / jnp.sqrt(pbox[e] * pbox[b] + EPSILON)
        real = real * root
        imag = imag * root
        factor = weight * (real * real + imag * imag)
        factors[e * (OFFS + 1) + distance] = factor
        weighted = factor * (imag - (est[e] - est[b]))
        acc[e] = acc[e] + weighted
        acc[b] = acc[b] - weighted

    def pairs_of(b):
        @pl.loop(lax.max(b - OFFS, 0), lax.min(b, here))
        def _(e):
            pair(e, b)

    def settle(b):
        k = b - here
        c_rim(b).wait_recv()
        prepare(b)
        z_est(k).wait_recv()
        pairs_of(b)
        own_low[k] = acc[k].astype(BF16)
        returned(k).start()
        owned(k).start()

    @pl.loop(0, here)
    def _(b):
        tile_in(b).wait()
        x_wait(b, True)
        c_rim(b).start()

        @pl.when(b > 0)
        def _():
            c_rim(b - 1).wait_recv()
            prepare(b - 1)
            pairs_of(b - 1)

    c_rim(here - 1).wait_recv()
    prepare(here - 1)
    pairs_of(here - 1)

    @pl.loop(0, OFFS)
    def _(k):
        b = k + here
        z_tile(k).wait_recv()
        x_start(b, False)

        @pl.when(k > 0)
        def _():
            settle(b - 1)

        x_wait(b, False)
        c_rim(b).start()

    settle(everything - 1)

    z_dir().wait_recv()
    dirs[pl.ds(here, OFFS)] = dir_in[...].astype(F32)
    zero = jnp.zeros((8, LANES), F32)

    @pl.loop(OFFS, here)
    def _(k):
        grad[k] = acc[k]
        gradient[k] = acc[k]

    @pl.loop(0, OFFS)
    def _(k):
        returned(k).wait_recv()
        owned(k).wait_recv()
        whole = acc[k] + ret_in[k]
        grad[k] = whole
        gradient[k] = whole
        grad[here + k] = own_in[k].astype(F32) + acc[here + k]

    def one_epoch(e, sums):
        norm, crossed, gg, gd, dd = sums
        g = grad[e]
        d = dirs[e]
        norm = norm + folded(g * g)
        crossed = crossed + folded(g * d)
        for slot in range(SLOTS):
            far = offsets[e, slot]
            f = factors[e * (OFFS + 1) + far]
            dg = g - grad[e + far]
            ds = d - dirs[e + far]
            fg = f * dg
            gg = gg + folded(fg * dg)
            gd = gd + folded(fg * ds)
            dd = dd + folded(f * ds * ds)
        return norm, crossed, gg, gd, dd

    sums = lax.fori_loop(0, here, one_epoch, (zero,) * 5)
    tile_row = lax.broadcasted_iota(jnp.int32, (8, LANES), 0)
    tile = zero
    for index, value in enumerate(sums):
        whole = jnp.sum(jnp.sum(value, axis=0, keepdims=True), axis=1, keepdims=True)
        tile = jnp.where(tile_row == index, whole, tile)

    for size, me, peer, red, send, recv in (
        (spread, place, in_plane, red_s, rs_send, rs_recv),
        (nz, z, along_z, red_z, rz_send, rz_recv),
    ):
        if size == 1:
            continue
        red[me] = tile

        def share(by, source):
            return remote(
                red.at[source], red.at[source], send.at[by], recv.at[source], peer(by)
            )

        for by in range(1, size):
            share(by, me).start()
        for by in range(1, size):
            share(by, lax.rem(me + size - by, size)).wait_recv()
        for by in range(1, size):
            share(by, me).wait_send()
        tile = red[0]
        for source in range(1, size):
            tile = tile + red[source]
    totals[...] = tile

    @pl.loop(0, OFFS)
    def _(k):
        z_tile(k).wait_send()
        z_est(k).wait_send()
        returned(k).wait_send()
        owned(k).wait_send()

    @pl.loop(0, here)
    def _(b):
        x_drain(b, True)

    @pl.loop(here, everything)
    def _(b):
        x_drain(b, False)

    @pl.loop(0, everything)
    def _(b):
        c_rim(b).wait_send()

    z_dir().wait_send()


def on_device(sizes, slc, offsets, weights, estimate, direction, prev_mean):
    nz, nx, nc = sizes
    here, rows, cols = slc.shape[1:]
    look_rows = rows // LOOK
    every = here + OFFS
    total_rows = rows + 2 * PACK
    ext_rows = total_rows // LOOK
    wide = cols + LANES
    grid_cell = (look_rows, cols)
    dma = pltpu.SemaphoreType.DMA
    scratch = [
        pltpu.SMEM(offsets.shape, jnp.int32),
        pltpu.SMEM(weights.shape, F32),
        pltpu.VMEM((every, 2, total_rows, wide), BF16),
        pltpu.VMEM((2, wide // LANES, total_rows, LANES), F32),
        pltpu.VMEM((every, 2, LOOK, ext_rows, wide), F32),
        pltpu.VMEM((every,) + grid_cell, F32),
        pltpu.VMEM((every,) + grid_cell, F32),
        pltpu.VMEM((every,) + grid_cell, F32),
        pltpu.VMEM((OFFS,) + grid_cell, BF16),
        pltpu.VMEM((OFFS,) + grid_cell, BF16),
        pltpu.VMEM((every,) + grid_cell, F32),
        pltpu.VMEM((OFFS,) + grid_cell, F32),
        pltpu.VMEM((OFFS,) + grid_cell, BF16),
        pltpu.VMEM((OFFS,) + grid_cell, BF16),
        pltpu.VMEM((every,) + grid_cell, F32),
        pltpu.VMEM((here * (OFFS + 1),) + grid_cell, F32),
        pltpu.VMEM((nx * nc, 8, LANES), F32),
        pltpu.VMEM((nz, 8, LANES), F32),
        dma((here,)),
        dma((4,)),
        dma((OFFS,)),
        dma((OFFS,)),
        dma((OFFS,)),
        dma((OFFS,)),
        dma((2,)),
        dma((2, every)),
        dma((2, every)),
        dma((every,)),
        dma((every,)),
        dma((OFFS,)),
        dma((OFFS,)),
        dma((OFFS,)),
        dma((OFFS,)),
        dma((nx * nc,)),
        dma((nx * nc,)),
        dma((nz,)),
        dma((nz,)),
    ]
    anywhere = pl.BlockSpec(memory_space=pl.ANY)
    vectors = pl.BlockSpec(memory_space=pltpu.VMEM)
    gradient, totals = pl.pallas_call(
        functools.partial(step_kernel, sizes),
        name="cg_step",
        out_shape=(
            jax.ShapeDtypeStruct(estimate.shape, F32),
            jax.ShapeDtypeStruct((8, LANES), F32),
        ),
        in_specs=[anywhere] * 5,
        out_specs=(vectors, vectors),
        scratch_shapes=scratch,
        compiler_params=pltpu.CompilerParams(
            collective_id=0, has_side_effects=True, vmem_limit_bytes=60 * 1024 * 1024
        ),
    )(slc, offsets, weights, estimate, direction)
    grad_norm, crossed, grad_term, mixed_term, old_term = (totals[i, 0] for i in range(5))
    cell_count = float(estimate.size * nz * nx * nc)
    momentum = grad_norm / cell_count / prev_mean[0]
    curvature = grad_term + 2.0 * momentum * mixed_term + momentum * momentum * old_term
    step = (grad_norm + momentum * crossed) / curvature
    moved = gradient + momentum * direction
    return (estimate + step * moved, moved)


def solution(mesh):
    sizes = (mesh.shape["epoch"], mesh.shape["space"], mesh.shape["sub"])
    tile = P(("groups", "epoch"), "space", "sub")
    rows = P(("groups", "epoch"), None)
    return jax.shard_map(
        functools.partial(on_device, sizes),
        mesh=mesh,
        in_specs=(P(None, ("groups", "epoch"), "space", "sub"), rows, rows, tile, tile, P()),
        out_specs=(tile, tile),
        check_vma=False,
    )
```

```python
import functools

import jax
import jax.numpy as jnp
from jax import lax
from jax.experimental import pallas as pl
from jax.experimental.pallas import tpu as pltpu
from jax.sharding import PartitionSpec as P

SLOTS = 4
OFFS = 8
LOOK = 4
RADIUS = 3
EPSILON = 1e-06
LANES = 128
LAG = 3
PACK = 16
MESH = pl.DeviceIdType.MESH
F32 = jnp.float32
BF16 = jnp.bfloat16


def windowed(x, axis):
    size = x.shape[axis]
    three = x + pltpu.roll(x, 1, axis) + pltpu.roll(x, size - 1, axis)
    return x + pltpu.roll(three, 2, axis) + pltpu.roll(three, size - 2, axis)


def folded(x):
    total = None
    for row in range(0, x.shape[0], 8):
        for col in range(0, x.shape[1], LANES):
            piece = x[row : row + 8, col : col + LANES]
            total = piece if total is None else total + piece
    return total


def step_kernel(
    sizes,
    slc,
    offsets_in,
    weights_in,
    estimate,
    direction,
    prev_mean,
    gradient,
    momenta,
    steps,
    offsets,
    weights,
    raw,
    tmp,
    ext,
    pbox,
    est,
    dirs,
    dir_low,
    dir_in,
    acc,
    ret_in,
    own_low,
    own_in,
    grad,
    factors,
    red_s,
    red_z,
    loc_sem,
    misc_sem,
    z_send,
    z_recv,
    e_send,
    e_recv,
    d_sem,
    x_send,
    x_recv,
    c_send,
    c_recv,
    r_send,
    r_recv,
    o_send,
    o_recv,
    rs_send,
    rs_recv,
    rz_send,
    rz_recv,
):
    nz, nx, nc = sizes
    here = slc.shape[1]
    rows = slc.shape[2]
    cols = slc.shape[3]
    total_rows = rows + 2 * PACK
    look_rows = rows // LOOK
    ext_rows = total_rows // LOOK
    rim_rows = PACK // LOOK
    blocks = cols // LANES + 1
    everything = here + OFFS
    z = lax.axis_index("epoch")
    x = lax.axis_index("space")
    c = lax.axis_index("sub")
    z_prev = {"epoch": lax.rem(z + nz - 1, nz)}
    z_next = {"epoch": lax.rem(z + 1, nz)}
    has_next = x < nx - 1
    has_prev = x > 0

    local = [
        pltpu.make_async_copy(estimate, est.at[pl.ds(0, here)], misc_sem.at[0]),
        pltpu.make_async_copy(direction, dirs.at[pl.ds(0, here)], misc_sem.at[1]),
        pltpu.make_async_copy(offsets_in, offsets, misc_sem.at[2]),
        pltpu.make_async_copy(weights_in, weights, misc_sem.at[3]),
    ]

    def tile_in(b):
        return pltpu.make_async_copy(
            slc.at[:, b], raw.at[b, :, pl.ds(0, rows), pl.ds(0, cols)], loc_sem.at[b]
        )

    local[1].start()
    local[0].start()
    local[2].start()
    local[3].start()
    for b in range(here):
        tile_in(b).start()

    barrier = pltpu.get_barrier_semaphore()
    spread = nx * nc
    place = x * nc + c

    def along_z(by):
        return {"epoch": lax.rem(z + by, nz)}

    def in_plane(by):
        other = lax.rem(place + by, spread)
        return {"space": other // nc, "sub": lax.rem(other, nc)}

    for by in range(1, nz):
        pl.semaphore_signal(barrier, inc=1, device_id=along_z(by), device_id_type=MESH)
    for by in range(1, spread):
        pl.semaphore_signal(barrier, inc=1, device_id=in_plane(by), device_id_type=MESH)
    pl.semaphore_wait(barrier, nz + spread - 2)

    def remote(src, dst, send, recv, device):
        return pltpu.make_async_remote_copy(
            src_ref=src,
            dst_ref=dst,
            send_sem=send,
            recv_sem=recv,
            device_id=device,
            device_id_type=MESH,
        )

    def z_tile(k):
        return remote(
            slc.at[:, k],
            raw.at[here + k, :, pl.ds(0, rows), pl.ds(0, cols)],
            z_send.at[k],
            z_recv.at[k],
            z_prev,
        )

    def z_est(k):
        return remote(estimate.at[k], est.at[here + k], e_send.at[k], e_recv.at[k], z_prev)

    def z_dir():
        return remote(dir_low, dir_in, d_sem.at[0], d_sem.at[1], z_prev)

    def x_down(b, own):
        at = pl.ds(rows - PACK, PACK)
        src = slc.at[:, b, at] if own else raw.at[b, :, at, pl.ds(0, cols)]
        return remote(
            src,
            raw.at[b, :, pl.ds(rows + PACK, PACK), pl.ds(0, cols)],
            x_send.at[0, b],
            x_recv.at[0, b],
            {"space": lax.rem(x + 1, nx)},
        )

    def x_up(b, own):
        at = pl.ds(0, PACK)
        src = slc.at[:, b, at] if own else raw.at[b, :, at, pl.ds(0, cols)]
        return remote(
            src,
            raw.at[b, :, pl.ds(rows, PACK), pl.ds(0, cols)],
            x_send.at[1, b],
            x_recv.at[1, b],
            {"space": lax.rem(x + nx - 1, nx)},
        )

    def c_rim(b):
        start = pl.multiple_of((nc - 1 - c) * (cols - LANES), LANES)
        return remote(
            raw.at[b, :, :, pl.ds(start, LANES)],
            raw.at[b, :, :, pl.ds(cols, LANES)],
            c_send.at[b],
            c_recv.at[b],
            {"sub": lax.rem(c + 1, nc)},
        )

    def x_start(b, own):
        if nx > 1:
            pl.when(has_next)(lambda: x_down(b, own).start())
            pl.when(has_prev)(lambda: x_up(b, own).start())

    def x_wait(b, own):
        if nx > 1:
            pl.when(has_prev)(lambda: x_down(b, own).wait_recv())
            pl.when(has_next)(lambda: x_up(b, own).wait_recv())

    def x_drain(b, own):
        if nx > 1:
            pl.when(has_next)(lambda: x_down(b, own).wait_send())
            pl.when(has_prev)(lambda: x_up(b, own).wait_send())

    def returned(k):
        return remote(acc.at[here + k], ret_in.at[k], r_send.at[k], r_recv.at[k], z_next)

    def owned(k):
        return remote(own_low.at[k], own_in.at[k], o_send.at[k], o_recv.at[k], z_prev)

    for k in range(OFFS):
        x_start(k, True)
    for k in range(OFFS + LAG):
        if k < OFFS:
            z_tile(k).start()
        if k >= LAG:
            z_est(k - LAG).start()
    local[1].wait()
    dir_low[...] = dirs[pl.ds(0, OFFS)].astype(BF16)
    acc[...] = jnp.zeros_like(acc)
    for copy in (local[0], local[2], local[3]):
        copy.wait()
    z_dir().start()

    row_at = lax.broadcasted_iota(jnp.int32, (ext_rows, LANES), 0)
    lane_at = lax.broadcasted_iota(jnp.int32, (ext_rows, LANES), 1)
    row_first = jnp.where(has_prev, look_rows + rim_rows, ext_rows)
    row_last = jnp.where(has_next, look_rows + rim_rows, look_rows)
    row_ok = (row_at < row_last) | (row_at >= row_first)
    if nc > 1:
        lane_first = jnp.where(c == 0, LANES, LANES - RADIUS)
        lane_last = jnp.where(c == 0, RADIUS, 0)
        rim_ok = row_ok & ((lane_at < lane_last) | (lane_at >= lane_first))
    else:
        rim_ok = row_at < 0

    def boxed(field):
        return windowed(windowed(field, 0)[:look_rows], 1)[:, :cols]

    def prepare(b):
        for part in range(2):
            for v in range(blocks):
                tmp[part, v] = raw[b, part, :, v * LANES : (v + 1) * LANES].astype(F32)
        powers = []
        for v in range(blocks):
            keep = rim_ok if v == blocks - 1 else row_ok
            power = jnp.zeros((ext_rows, LANES), F32)
            for part in range(2):
                for look in range(LOOK):
                    value = tmp[part, v, pl.ds(look, ext_rows, stride=LOOK), :]
                    value = jnp.where(keep, value, 0.0)
                    ext[b, part, look, :, v * LANES : (v + 1) * LANES] = value
                    power = power + value * value
            powers.append(power)
        pbox[b] = boxed(jnp.concatenate(powers, axis=1))

    def pair(e, b):
        real = jnp.zeros((ext_rows, blocks * LANES), F32)
        imag = jnp.zeros((ext_rows, blocks * LANES), F32)
        for look in range(LOOK):
            own_real = ext[e, 0, look]
            own_imag = ext[e, 1, look]
            mate_real = ext[b, 0, look]
            mate_imag = ext[b, 1, look]
            real = real + (own_real * mate_real + own_imag * mate_imag)
            imag = imag + (own_imag * mate_real - own_real * mate_imag)
        real = boxed(real)
        imag = boxed(imag)
        distance = b - e
        weight = jnp.float32(0.0)
        for slot in range(SLOTS):
            weight = weight + jnp.where(
                offsets[slot, e] == distance, weights[slot, e], jnp.float32(0.0)
            )
        root = 1.0 / jnp.sqrt(pbox[e] * pbox[b] + EPSILON)
        real = real * root
        imag = imag * root
        factor = weight * (real * real + imag * imag)
        factors[e * (OFFS + 1) + distance] = factor
        weighted = factor * (imag - (est[e] - est[b]))
        acc[e] = acc[e] + weighted
        acc[b] = acc[b] - weighted

    def pairs_of(b):
        @pl.loop(lax.max(b - OFFS, 0), lax.min(b, here))
        def _(e):
            pair(e, b)

    def settle(b):
        k = b - here
        c_rim(b).wait_recv()
        prepare(b)
        z_est(k).wait_recv()
        pairs_of(b)
        own_low[k] = acc[k].astype(BF16)
        returned(k).start()
        owned(k).start()

    @pl.loop(0, here)
    def _(b):
        tile_in(b).wait()
        x_wait(b, True)
        c_rim(b).start()

        @pl.when(b > 0)
        def _():
            c_rim(b - 1).wait_recv()
            prepare(b - 1)
            pairs_of(b - 1)

    c_rim(here - 1).wait_recv()
    prepare(here - 1)
    pairs_of(here - 1)

    @pl.loop(0, OFFS)
    def _(k):
        b = k + here
        z_tile(k).wait_recv()
        x_start(b, False)

        @pl.when(k > 0)
        def _():
            settle(b - 1)

        x_wait(b, False)
        c_rim(b).start()

    settle(everything - 1)

    z_dir().wait_recv()
    dirs[pl.ds(here, OFFS)] = dir_in[...].astype(F32)
    zero = jnp.zeros((8, LANES), F32)

    @pl.loop(OFFS, here)
    def _(k):
        grad[k] = acc[k]
        gradient[k] = acc[k]

    @pl.loop(0, OFFS)
    def _(k):
        returned(k).wait_recv()
        owned(k).wait_recv()
        whole = acc[k] + ret_in[k]
        grad[k] = whole
        gradient[k] = whole
        grad[here + k] = own_in[k].astype(F32) + acc[here + k]

    def one_epoch(e, sums):
        norm, crossed, gg, gd, dd = sums
        g = grad[e]
        d = dirs[e]
        norm = norm + folded(g * g)
        crossed = crossed + folded(g * d)
        for slot in range(SLOTS):
            far = offsets[slot, e]
            f = factors[e * (OFFS + 1) + far]
            dg = g - grad[e + far]
            ds = d - dirs[e + far]
            fg = f * dg
            gg = gg + folded(fg * dg)
            gd = gd + folded(fg * ds)
            dd = dd + folded(f * ds * ds)
        return norm, crossed, gg, gd, dd

    sums = lax.fori_loop(0, here, one_epoch, (zero,) * 5)
    tile_row = lax.broadcasted_iota(jnp.int32, (8, LANES), 0)
    tile = zero
    for index, value in enumerate(sums):
        whole = jnp.sum(jnp.sum(value, axis=0, keepdims=True), axis=1, keepdims=True)
        tile = jnp.where(tile_row == index, whole, tile)

    for size, me, peer, red, send, recv in (
        (spread, place, in_plane, red_s, rs_send, rs_recv),
        (nz, z, along_z, red_z, rz_send, rz_recv),
    ):
        if size == 1:
            continue
        red[me] = tile

        def share(by, source):
            return remote(
                red.at[source], red.at[source], send.at[by], recv.at[source], peer(by)
            )

        for by in range(1, size):
            share(by, me).start()
        for by in range(1, size):
            share(by, lax.rem(me + size - by, size)).wait_recv()
        for by in range(1, size):
            share(by, me).wait_send()
        tile = red[0]
        for source in range(1, size):
            tile = tile + red[source]
    grad_norm, crossed, grad_term, mixed_term, old_term = (tile[i : i + 1, 0:1] for i in range(5))
    cell_count = float(here * look_rows * cols * nz * nx * nc)
    momentum = grad_norm / cell_count / prev_mean[0]
    curvature = grad_term + 2.0 * momentum * mixed_term + momentum * momentum * old_term
    momenta[...] = jnp.broadcast_to(momentum, momenta.shape)
    steps[...] = jnp.broadcast_to((grad_norm + momentum * crossed) / curvature, steps.shape)

    @pl.loop(0, OFFS)
    def _(k):
        z_tile(k).wait_send()
        z_est(k).wait_send()
        returned(k).wait_send()
        owned(k).wait_send()

    @pl.loop(0, here)
    def _(b):
        x_drain(b, True)

    @pl.loop(here, everything)
    def _(b):
        x_drain(b, False)

    @pl.loop(0, everything)
    def _(b):
        c_rim(b).wait_send()

    z_dir().wait_send()


def on_device(sizes, slc, offsets, weights, estimate, direction, prev_mean):
    nz, nx, nc = sizes
    here, rows, cols = slc.shape[1:]
    look_rows = rows // LOOK
    every = here + OFFS
    total_rows = rows + 2 * PACK
    ext_rows = total_rows // LOOK
    wide = cols + LANES
    grid_cell = (look_rows, cols)
    dma = pltpu.SemaphoreType.DMA
    scratch = [
        pltpu.SMEM(offsets.shape[::-1], jnp.int32),
        pltpu.SMEM(weights.shape[::-1], F32),
        pltpu.VMEM((every, 2, total_rows, wide), BF16),
        pltpu.VMEM((2, wide // LANES, total_rows, LANES), F32),
        pltpu.VMEM((every, 2, LOOK, ext_rows, wide), F32),
        pltpu.VMEM((every,) + grid_cell, F32),
        pltpu.VMEM((every,) + grid_cell, F32),
        pltpu.VMEM((every,) + grid_cell, F32),
        pltpu.VMEM((OFFS,) + grid_cell, BF16),
        pltpu.VMEM((OFFS,) + grid_cell, BF16),
        pltpu.VMEM((every,) + grid_cell, F32),
        pltpu.VMEM((OFFS,) + grid_cell, F32),
        pltpu.VMEM((OFFS,) + grid_cell, BF16),
        pltpu.VMEM((OFFS,) + grid_cell, BF16),
        pltpu.VMEM((every,) + grid_cell, F32),
        pltpu.VMEM((here * (OFFS + 1),) + grid_cell, F32),
        pltpu.VMEM((nx * nc, 8, LANES), F32),
        pltpu.VMEM((nz, 8, LANES), F32),
        dma((here,)),
        dma((4,)),
        dma((OFFS,)),
        dma((OFFS,)),
        dma((OFFS,)),
        dma((OFFS,)),
        dma((2,)),
        dma((2, every)),
        dma((2, every)),
        dma((every,)),
        dma((every,)),
        dma((OFFS,)),
        dma((OFFS,)),
        dma((OFFS,)),
        dma((OFFS,)),
        dma((nx * nc,)),
        dma((nx * nc,)),
        dma((nz,)),
        dma((nz,)),
    ]
    anywhere = pl.BlockSpec(memory_space=pl.ANY)
    vectors = pl.BlockSpec(memory_space=pltpu.VMEM)
    gradient, momenta, steps = pl.pallas_call(
        functools.partial(step_kernel, sizes),
        name="cg_step",
        out_shape=(
            jax.ShapeDtypeStruct(estimate.shape, F32),
            jax.ShapeDtypeStruct((1,) + grid_cell, F32),
            jax.ShapeDtypeStruct((1,) + grid_cell, F32),
        ),
        in_specs=[anywhere] * 5 + [pl.BlockSpec(memory_space=pltpu.SMEM)],
        out_specs=(vectors, vectors, vectors),
        scratch_shapes=scratch,
        compiler_params=pltpu.CompilerParams(
            collective_id=0, has_side_effects=True, vmem_limit_bytes=60 * 1024 * 1024
        ),
    )(slc, offsets.T, weights.T, estimate, direction, prev_mean)
    moved = gradient + momenta * direction
    return (estimate + steps * moved, moved)


def solution(mesh):
    sizes = (mesh.shape["epoch"], mesh.shape["space"], mesh.shape["sub"])
    tile = P(("groups", "epoch"), "space", "sub")
    rows = P(("groups", "epoch"), None)
    return jax.shard_map(
        functools.partial(on_device, sizes),
        mesh=mesh,
        in_specs=(P(None, ("groups", "epoch"), "space", "sub"), rows, rows, tile, tile, P()),
        out_specs=(tile, tile),
        check_vma=False,
    )
```
